32 devices in a mesh: grp: 2 (over y), row: 4 (over x, core), col: 4 (over z).
Axes of the slice: x: 2, y: 2, z: 4, core: 2. Of those that a mesh axis runs over, the one named last changes fastest.
Arguments:
- programs: bfloat16 [2048, 2048], P(('grp', 'row'), 'col'), parts along dimension 0, may hold values from -6 to 6
- tests: bfloat16 [2048, 2048], P(('grp', 'col'), 'row'), parts along dimension 0, may hold values from -6 to 6
- weight: bfloat16 [2048, 2048], P('col', 'row'), may hold values from -0.125 to 0.125
- labels: int32 [2048, 1024], P(('grp', 'row'), 'col'), parts along dimension 0, may hold values 0 or 1
Outputs:
- grad_programs: bfloat16 [2048, 2048], P(('grp', 'row'), 'col'), parts along dimension 0
- grad_tests: bfloat16 [2048, 2048], P(('grp', 'col'), 'row'), parts along dimension 0
- grad_weight: float32 [4096, 2048], P(('grp', 'col'), 'row'), parts along dimension 0
The draws below stay inside these ranges and needn't reach their ends.
There are 2 independent parts, one for each index of `grp`. The reference program is written for one: setup_inputs(seed, part) draws one part's arguments, and reference() takes and returns one part's arrays. A program takes and returns all parts, laid end to end along the dimension named above; an argument that names none is the same for every part. Nothing has to cross between parts.
All inputs are finite; a program needn't handle non-finite values. No bound on the sum of `labels` on one device may be relied on, other than what follows from the above.
Results may differ from the reference program's by a relative error of at most 0.017.
Values may be sent and summed in bfloat16 or wider, within the bound.
A program may use at most 64 MiB of HBM per device.

```python
import math
import jax
import jax.numpy as jnp

E = 2048
NP = 1024
NT = 1024


def plant(values, stream_key, least, high):
    index_at = [jax.random.randint(jax.random.fold_in(stream_key, axis), (), 0, length) for axis, length in enumerate(values.shape)]
    main_axis = values.shape.index(max(values.shape))
    beside = index_at[:main_axis] + [(index_at[main_axis] + 1) % values.shape[main_axis]] + index_at[main_axis + 1:]
    return values.at[tuple(index_at)].set(least).at[tuple(beside)].set(high)


def block_scale(stream_key, dims, pieces, low, high):
    loudness, own = 1.0, jax.random.fold_in(stream_key, 6)
    for position, blocks in pieces:
        steps = jnp.exp(jax.random.uniform(jax.random.fold_in(own, position), (blocks,), jnp.float32, low / len(pieces), high / len(pieces)))
        loudness = loudness * jnp.repeat(steps, dims[position] // blocks).reshape([-1 if axis == position else 1 for axis in range(len(dims))])
    return loudness


def scatter_about(key, dims, spread, limit, shards=(), kind=jnp.bfloat16):
    level = block_scale(key, dims, shards, -0.22, 0.18) if shards else 1.0
    drawn = jax.random.normal(key, dims, jnp.float32) * spread * level
    return jnp.minimum(jnp.maximum(drawn, -limit), limit).astype(kind)


def setup_inputs(seed: int = 0, part: int = 0) -> dict:
    key_list = jax.random.split(jax.random.key(seed), 5)
    part_splits = jax.random.split(jax.random.fold_in(key_list[4], part), 5)
    return {
        "programs": scatter_about(part_splits[0], (NP, E), 1.0, 6.0, ((0, 4), (1, 4))),
        "tests": scatter_about(part_splits[1], (NT, E), 1.0, 6.0, ((0, 4), (1, 4))),
        "weight": scatter_about(key_list[2], (E, E), E ** -0.5, 0.125, ((0, 4), (1, 4))),
        "labels": plant((jax.random.randint(part_splits[3], (NP, NT), 0, 2) < 1).astype(jnp.int32), jax.random.fold_in(part_splits[3], 1), 0, 1),
    }


def reference(programs, tests, weight, labels):
    factor = 1.0 / math.sqrt(E)
    projected = jnp.dot(programs, weight, preferred_element_type=jnp.float32).astype(jnp.bfloat16)
    logits = jnp.dot(projected, tests.T, preferred_element_type=jnp.float32) * factor
    dlogits = (jax.nn.sigmoid(logits) - labels.astype(jnp.float32)).astype(jnp.bfloat16)
    test_sums = jnp.dot(dlogits, tests, preferred_element_type=jnp.float32).astype(jnp.bfloat16)
    grad_programs = (jnp.dot(test_sums, weight.T, preferred_element_type=jnp.float32) * factor).astype(jnp.bfloat16)
    grad_weight = jnp.dot(programs.T, test_sums, preferred_element_type=jnp.float32) * factor
    grad_tests = (jnp.dot(dlogits.T, projected, preferred_element_type=jnp.float32) * factor).astype(jnp.bfloat16)
    return (grad_programs, grad_tests, grad_weight)
```

```python
import functools
import math

import jax
import jax.numpy as jnp
from jax import lax
from jax.experimental import pallas as pl
from jax.experimental.pallas import tpu as pltpu
from jax.sharding import PartitionSpec as P

E = 2048
MESH = pl.DeviceIdType.MESH
BF16 = jnp.bfloat16
F32 = jnp.float32


def contract(left, right, left_dim, right_dim):
    return lax.dot_general(
        left, right, (((left_dim,), (right_dim,)), ((), ())), preferred_element_type=F32
    )


def partner(index, step):
    bit = 1
    while bit <= step:
        if step & bit:
            index = index + bit - 2 * bit * (lax.div(index, bit) % 2)
        bit *= 2
    return index


def each(count, body):
    if count <= 4:
        for k in range(1, count):
            body(k)
    else:
        lax.fori_loop(1, count, lambda k, x: (body(k), x)[1], 0)


def kernel(
    rows, cols,
    p_ref, t_ref, w_ref, l_ref,
    gp_ref, gt_ref, gw_ref,
    t_all, m_part, m_recv, m_all, l_part, l_recv, d_all, q_part, q_recv, q_all, g_part, g_recv,
    acc, send, recv,
):
    factor = 1.0 / math.sqrt(E)
    r, c = lax.axis_index("row"), lax.axis_index("col")
    t_send, ms_send, ma_send, l_send, d_send, qs_send, qa_send, g_send = (send.at[i] for i in range(8))
    t_recv, ms_recv, ma_recv, lr_recv, d_recv, qs_recv, qa_recv, gr_recv = (recv.at[i] for i in range(8))
    sub = m_part.shape[2]

    def row_peer(k):
        return {"row": lax.rem(r + k, rows)}

    def col_peer(s):
        return {"col": partner(c, s)}

    barrier = pltpu.get_barrier_semaphore()
    each(rows, lambda k: pl.semaphore_signal(barrier, inc=1, device_id=row_peer(k), device_id_type=MESH))
    for s in range(1, cols):
        pl.semaphore_signal(barrier, inc=1, device_id=col_peer(s), device_id_type=MESH)
    pl.semaphore_wait(barrier, rows - 1 + cols - 1)

    def copy_col(src, dst, s, ssem, rsem):
        return pltpu.make_async_remote_copy(
            src_ref=src, dst_ref=dst, send_sem=ssem.at[s], recv_sem=rsem.at[s],
            device_id=col_peer(s), device_id_type=MESH,
        )

    def drain(ref, sem):
        pltpu.make_async_copy(ref, ref, sem).wait()

    for s in range(1, cols):
        copy_col(t_ref, t_all.at[s - 1], s, t_send, t_recv).start()

    def scatter(part, into, s, ssem, rsem):
        def one(k):
            pltpu.make_async_remote_copy(
                src_ref=part.at[s, lax.rem(r + k, rows)], dst_ref=into.at[s, k - 1],
                send_sem=ssem.at[s], recv_sem=rsem.at[s],
                device_id=row_peer(k), device_id_type=MESH,
            ).start()
        each(rows, one)

    def gather(full, s, ssem, rsem):
        def one(k):
            pltpu.make_async_remote_copy(
                src_ref=full.at[s, r], dst_ref=full.at[s, r],
                send_sem=ssem.at[s], recv_sem=rsem.at[s],
                device_id=row_peer(k), device_id_type=MESH,
            ).start()
        each(rows, one)

    def reduce_share(part, came, full, s, ssem, rsem, rs_sem):
        drain(came.at[s], rs_sem.at[s])
        total = part[s, r].astype(F32)
        for k in range(rows - 1):
            total = total + came[s, k].astype(F32)
        full[s, r] = total.astype(BF16)
        gather(full, s, ssem, rsem)

    def whole(full, s):
        return full[s].reshape(rows * sub, full.shape[3])

    def tests_of(s):
        return t_ref[...] if s == 0 else t_all[s - 1]

    def m_make(s):
        if s:
            drain(t_all.at[s - 1], t_recv.at[s])
        part = contract(tests_of(s), w_ref[...], 1, 1)
        m_part[s] = part.astype(BF16).reshape(m_part.shape[1:])
        scatter(m_part, m_recv, s, ms_send, ms_recv)

    def m_sum(s):
        reduce_share(m_part, m_recv, m_all, s, ma_send, ma_recv, ms_recv)

    def m_use(s):
        drain(m_all.at[s, pl.ds(0, rows - 1)], ma_recv.at[s])
        part = contract(p_ref[...], whole(m_all, s), 1, 1)
        if s == 0:
            acc[...] = part
        else:
            l_part[s - 1] = part.astype(BF16)
            copy_col(l_part.at[s - 1], l_recv.at[s - 1], s, l_send, lr_recv).start()

    for s in range(cols + 2):
        if s < cols:
            m_make(s)
        if 0 <= s - 1 < cols:
            m_sum(s - 1)
        if 0 <= s - 2 < cols:
            m_use(s - 2)

    logits = acc[...]
    for s in range(1, cols):
        drain(l_recv.at[s - 1], lr_recv.at[s])
        logits = logits + l_recv[s - 1].astype(F32)
    d_all[0] = (jax.nn.sigmoid(logits * factor) - l_ref[...].astype(F32)).astype(BF16)
    for s in range(1, cols):
        copy_col(d_all.at[0], d_all.at[s], s, d_send, d_recv).start()

    def q_make(s):
        if s:
            drain(d_all.at[s], d_recv.at[s])
        part = contract(d_all[s], p_ref[...], 0, 0)
        q_part[s] = part.astype(BF16).reshape(q_part.shape[1:])
        scatter(q_part, q_recv, s, qs_send, qs_recv)

    def q_sum(s):
        reduce_share(q_part, q_recv, q_all, s, qa_send, qa_recv, qs_recv)

    def q_use(s):
        drain(q_all.at[s, pl.ds(0, rows - 1)], qa_recv.at[s])
        part = contract(whole(q_all, s), w_ref[...], 1, 0)
        if s == 0:
            g_part[0] = part.astype(BF16)
        else:
            g_part[s] = part.astype(BF16)
            copy_col(g_part.at[s], g_recv.at[s - 1], s, g_send, gr_recv).start()

    for s in range(cols + 2):
        if s < cols:
            q_make(s)
        if 0 <= s - 1 < cols:
            q_sum(s - 1)
        if 0 <= s - 2 < cols:
            q_use(s - 2)

    total = contract(d_all[0], whole(m_all, 0), 1, 0)
    for s in range(1, cols):
        total = total + contract(d_all[s], whole(m_all, s), 1, 0)
    gp_ref[...] = (total * factor).astype(BF16)
    total = contract(whole(q_all, 0), tests_of(0), 0, 0)
    for s in range(1, cols):
        total = total + contract(whole(q_all, s), tests_of(s), 0, 0)
    gw_ref[...] = total * factor

    total = g_part[0].astype(F32)
    for s in range(1, cols):
        drain(g_recv.at[s - 1], gr_recv.at[s])
        total = total + g_recv[s - 1].astype(F32)
    gt_ref[...] = (total * factor).astype(BF16)

    for s in range(cols):
        for full, sc, ga in ((m_all, ms_send, ma_send), (q_all, qs_send, qa_send)):
            drain(full.at[s, pl.ds(0, rows - 1)], sc.at[s])
            drain(full.at[s, pl.ds(0, rows - 1)], ga.at[s])
        if s:
            drain(t_ref, t_send.at[s])
            drain(l_part.at[s - 1], l_send.at[s])
            drain(d_all.at[0], d_send.at[s])
            drain(g_part.at[s], g_send.at[s])


def local(rows, cols, programs, tests, weight, labels):
    (pr, eb), (tb, fb) = programs.shape, tests.shape
    sub = tb // rows
    vmem = pl.BlockSpec(memory_space=pltpu.VMEM)
    block = lambda *shape: pltpu.VMEM(shape, BF16)
    return pl.pallas_call(
        functools.partial(kernel, rows, cols),
        out_shape=(
            jax.ShapeDtypeStruct((pr, eb), BF16),
            jax.ShapeDtypeStruct((tb, fb), BF16),
            jax.ShapeDtypeStruct((eb, fb), F32),
        ),
        in_specs=[vmem] * 4,
        out_specs=(vmem,) * 3,
        scratch_shapes=[
            block(cols - 1, tb, fb),
            block(cols, rows, sub, eb), block(cols, rows - 1, sub, eb), block(cols, rows, sub, eb),
            block(cols - 1, pr, tb), block(cols - 1, pr, tb),
            block(cols, pr, tb),
            block(cols, rows, sub, eb), block(cols, rows - 1, sub, eb), block(cols, rows, sub, eb),
            block(cols, tb, fb), block(cols - 1, tb, fb),
            pltpu.VMEM((pr, tb), F32),
            pltpu.SemaphoreType.DMA((8, cols)),
            pltpu.SemaphoreType.DMA((8, cols)),
        ],
        compiler_params=pltpu.CompilerParams(
            collective_id=0, has_side_effects=True, vmem_limit_bytes=48 * 1024 * 1024
        ),
    )(programs, tests, weight, labels)


def solution(mesh):
    placed = (
        P(("grp", "row"), "col"),
        P(("grp", "col"), "row"),
        P("col", "row"),
        P(("grp", "row"), "col"),
    )
    return jax.shard_map(
        functools.partial(local, mesh.shape["row"], mesh.shape["col"]),
        mesh=mesh,
        in_specs=placed,
        out_specs=(P(("grp", "row"), "col"), P(("grp", "col"), "row"), P(("grp", "col"), "row")),
        check_vma=False,
    )
```

```python
import functools
import math

import jax
import jax.numpy as jnp
from jax import lax
from jax.experimental import pallas as pl
from jax.experimental.pallas import tpu as pltpu
from jax.sharding import PartitionSpec as P

E = 2048
MESH = pl.DeviceIdType.MESH
BF16 = jnp.bfloat16
F32 = jnp.float32
M_ORDER = (0, 2, 1, 3)
D_SEND = (2, 1, 3)
Q_ORDER = (2, 1, 3, 0)


def contract(left, right, left_dim, right_dim):
    return lax.dot_general(
        left, right, (((left_dim,), (right_dim,)), ((), ())), preferred_element_type=F32
    )


def partner(index, step):
    bit = 1
    while bit <= step:
        if step & bit:
            index = index + bit - 2 * bit * (lax.div(index, bit) % 2)
        bit *= 2
    return index


def kernel(
    rows, cols,
    p_hbm, t_hbm, w_hbm, l_hbm,
    gp_ref, gt_ref, gw_ref,
    p_ref, w_ref, l_ref,
    t_all, m_part, m_sib, m_half, m_far, m_all, l_part, l_recv, d_all,
    q_part, q_sib, q_half, q_far, q_all, g_part, g_recv,
    acc, load, send, recv,
):
    factor = 1.0 / math.sqrt(E)
    r, c = lax.axis_index("row"), lax.axis_index("col")
    t_s, m1_s, m2_s, m3_s, l_s, d_s, q1_s, q2_s, q3_s, g_s = (send.at[i] for i in range(10))
    t_r, m1_r, m2_r, m3_r, l_r, d_r, q1_r, q2_r, q3_r, g_r = (recv.at[i] for i in range(10))
    core, chips = lax.rem(r, 2), rows // 2
    sibling = {"row": r + 1 - 2 * core}
    relay = cols == 4
    inner = lax.div(c + 1, 2) == 1

    loads = [
        pltpu.make_async_copy(a, b, load.at[i])
        for i, (a, b) in enumerate(((w_hbm, w_ref), (t_hbm, t_all.at[0]), (p_hbm, p_ref), (l_hbm, l_ref)))
    ]
    for one in loads:
        one.start()

    def far(k):
        return {"row": lax.rem(r + 2 * k, rows)}

    def col_peer(s):
        return {"col": partner(c, s)}

    barrier = pltpu.get_barrier_semaphore()
    for peer in [sibling] + [far(k) for k in range(1, chips)] + [col_peer(s) for s in range(1, cols)]:
        pl.semaphore_signal(barrier, inc=1, device_id=peer, device_id_type=MESH)
    pl.semaphore_wait(barrier, chips + cols - 1)

    def push(src, dst, ssem, rsem, peer):
        pltpu.make_async_remote_copy(
            src_ref=src, dst_ref=dst, send_sem=ssem, recv_sem=rsem, device_id=peer, device_id_type=MESH
        ).start()

    def drain(ref, sem):
        pltpu.make_async_copy(ref, ref, sem).wait()

    def send_tests(s):
        push(t_hbm, t_all.at[s], t_s.at[s], t_r.at[s], col_peer(s))

    if relay:
        send_tests(2)
        pl.when(inner)(lambda: send_tests(3))
        send_tests(1)
    else:
        for s in range(1, cols):
            send_tests(s)

    def share(value, part, s, ssem, rsem, sib):
        part[s] = value.astype(BF16).reshape(part.shape[1:])
        push(part.at[s, 1 - core], sib.at[s], ssem.at[s], rsem.at[s], sibling)

    def cross(part, sib, half, away, s, rsem1, ssem2, rsem2):
        drain(sib.at[s], rsem1.at[s])
        half[s] = (part[s, core].astype(F32) + sib[s].astype(F32)).astype(BF16)
        for k in range(1, chips):
            push(half.at[s], away.at[s, k - 1], ssem2.at[s], rsem2.at[s], far(k))

    def finish(half, away, full, s, rsem2, ssem3, rsem3):
        drain(away.at[s], rsem2.at[s])
        total = half[s].astype(F32)
        for k in range(chips - 1):
            total = total + away[s, k].astype(F32)
        full[s, core] = total.astype(BF16)
        push(full.at[s, core], full.at[s, core], ssem3.at[s], rsem3.at[s], sibling)

    def whole(full, s):
        return full[s].reshape(full.shape[1] * full.shape[2], full.shape[3])

    def m_make(s):
        if s:
            drain(t_all.at[s], t_r.at[s])
            if relay and s == 2:
                pl.when(inner)(lambda: push(t_all.at[2], t_all.at[3], t_s.at[0], t_r.at[3], col_peer(1)))
        share(contract(t_all[s], w_ref[...], 1, 1), m_part, s, m1_s, m1_r, m_sib)
        cross(m_part, m_sib, m_half, m_far, s, m1_r, m2_s, m2_r)

    def m_use(s):
        finish(m_half, m_far, m_all, s, m2_r, m3_s, m3_r)
        if s == 0:
            loads[2].wait()
        drain(m_half.at[s], m3_r.at[s])
        part = contract(p_ref[...], whole(m_all, s), 1, 1)
        if s == 0:
            acc[...] = part
        else:
            l_part[s - 1] = part.astype(BF16)
            push(l_part.at[s - 1], l_recv.at[s - 1], l_s.at[s], l_r.at[s], col_peer(s))

    loads[0].wait()
    loads[1].wait()
    order = M_ORDER if relay else list(range(cols))
    for i, s in enumerate(order):
        m_make(s)
        if i:
            m_use(order[i - 1])
    m_use(order[-1])

    loads[3].wait()
    logits = acc[...]
    for s in range(1, cols):
        drain(l_recv.at[s - 1], l_r.at[s])
        logits = logits + l_recv[s - 1].astype(F32)
    d_all[0] = (jax.nn.sigmoid(logits * factor) - l_ref[...].astype(F32)).astype(BF16)
    for s in (D_SEND if relay else range(1, cols)):
        push(d_all.at[0], d_all.at[s], d_s.at[s], d_r.at[s], col_peer(s))

    def q_make(s):
        if s:
            drain(d_all.at[s], d_r.at[s])
        share(contract(d_all[s], p_ref[...], 0, 0), q_part, s, q1_s, q1_r, q_sib)
        cross(q_part, q_sib, q_half, q_far, s, q1_r, q2_s, q2_r)

    def q_use(s):
        finish(q_half, q_far, q_all, s, q2_r, q3_s, q3_r)
        drain(q_half.at[s], q3_r.at[s])
        g_part[s] = contract(whole(q_all, s), w_ref[...], 1, 0).astype(BF16)
        if s:
            push(g_part.at[s], g_recv.at[s - 1], g_s.at[s], g_r.at[s], col_peer(s))

    order = Q_ORDER if relay else list(range(cols))
    for i, s in enumerate(order):
        q_make(s)
        if i:
            q_use(order[i - 1])
    q_use(order[-1])

    total = contract(d_all[0], whole(m_all, 0), 1, 0)
    for s in range(1, cols):
        total = total + contract(d_all[s], whole(m_all, s), 1, 0)
    gp_ref[...] = (total * factor).astype(BF16)
    total = contract(whole(q_all, 0), t_all[0], 0, 0)
    for s in range(1, cols):
        total = total + contract(whole(q_all, s), t_all[s], 0, 0)
    gw_ref[...] = total * factor

    total = g_part[0].astype(F32)
    for s in range(1, cols):
        drain(g_recv.at[s - 1], g_r.at[s])
        total = total + g_recv[s - 1].astype(F32)
    gt_ref[...] = (total * factor).astype(BF16)

    for s in range(cols):
        for away, half, s1, s2, s3 in ((m_far, m_half, m1_s, m2_s, m3_s), (q_far, q_half, q1_s, q2_s, q3_s)):
            drain(half.at[s], s1.at[s])
            drain(away.at[s], s2.at[s])
            drain(half.at[s], s3.at[s])
        if s:
            drain(l_part.at[s - 1], l_s.at[s])
            drain(d_all.at[0], d_s.at[s])
            drain(g_part.at[s], g_s.at[s])
            if not (relay and s == 3):
                drain(t_all.at[s], t_s.at[s])
    if relay:
        @pl.when(inner)
        def _():
            drain(t_all.at[3], t_s.at[3])
            drain(t_all.at[2], t_s.at[0])


def local(rows, cols, programs, tests, weight, labels):
    (pr, eb), (tb, fb) = programs.shape, tests.shape
    half, chips = tb // 2, rows // 2
    vmem, hbm = pl.BlockSpec(memory_space=pltpu.VMEM), pl.BlockSpec(memory_space=pl.ANY)
    block = lambda *shape: pltpu.VMEM(shape, BF16)
    reduce = [
        block(cols, 2, half, eb), block(cols, half, eb), block(cols, half, eb),
        block(cols, chips - 1, half, eb), block(cols, 2, half, eb),
    ]
    return pl.pallas_call(
        functools.partial(kernel, rows, cols),
        out_shape=(
            jax.ShapeDtypeStruct((pr, eb), BF16),
            jax.ShapeDtypeStruct((tb, fb), BF16),
            jax.ShapeDtypeStruct((eb, fb), F32),
        ),
        in_specs=[hbm] * 4,
        out_specs=(vmem,) * 3,
        scratch_shapes=[
            block(pr, eb), block(eb, fb), pltpu.VMEM((pr, tb), jnp.int32),
            block(cols, tb, fb),
            *reduce,
            block(cols - 1, pr, tb), block(cols - 1, pr, tb),
            block(cols, pr, tb),
            *reduce,
            block(cols, tb, fb), block(cols - 1, tb, fb),
            pltpu.VMEM((pr, tb), F32),
            pltpu.SemaphoreType.DMA((4,)),
            pltpu.SemaphoreType.DMA((10, cols)),
            pltpu.SemaphoreType.DMA((10, cols)),
        ],
        compiler_params=pltpu.CompilerParams(collective_id=0, has_side_effects=True),
    )(programs, tests, weight, labels)


def solution(mesh):
    placed = (
        P(("grp", "row"), "col"),
        P(("grp", "col"), "row"),
        P("col", "row"),
        P(("grp", "row"), "col"),
    )
    return jax.shard_map(
        functools.partial(local, mesh.shape["row"], mesh.shape["col"]),
        mesh=mesh,
        in_specs=placed,
        out_specs=(P(("grp", "row"), "col"), P(("grp", "col"), "row"), P(("grp", "col"), "row")),
        check_vma=False,
    )
```

```python
import functools
import math

import jax
import jax.numpy as jnp
from jax import lax
from jax.experimental import pallas as pl
from jax.experimental.pallas import tpu as pltpu
from jax.sharding import PartitionSpec as P

E = 2048
MESH = pl.DeviceIdType.MESH
BF16 = jnp.bfloat16
F32 = jnp.float32
M_ORDER = (0, 2, 1, 3)
Q_ORDER = (0, 2, 1, 3)
PARTS = 2
D_EARLY = 3
D_AFTER = 2


def contract(left, right, left_dim, right_dim):
    return lax.dot_general(
        left, right, (((left_dim,), (right_dim,)), ((), ())), preferred_element_type=F32
    )


def partner(index, step):
    bit = 1
    while bit <= step:
        if step & bit:
            index = index + bit - 2 * bit * (lax.div(index, bit) % 2)
        bit *= 2
    return index


def kernel(
    rows, cols,
    p_hbm, t_hbm, w_hbm, l_hbm,
    gp_ref, gt_ref, gw_ref,
    p_ref, w_ref, l_ref,
    t_all, m_part, m_sib, m_half, m_far, m_all, l_part, l_recv, d_all,
    q_part, q_sib, q_half, q_far, q_all, g_part, g_recv,
    acc, load, send, recv,
):
    factor = 1.0 / math.sqrt(E)
    r, c = lax.axis_index("row"), lax.axis_index("col")
    t_s, m1_s, m2_s, m3_s, l_s, d_s, q1_s, q2_s, q3_s, g_s = (send.at[i] for i in range(10))
    t_r, m1_r, m2_r, m3_r, l_r, d_r, q1_r, q2_r, q3_r, g_r = (recv.at[i] for i in range(10))
    core, chips = lax.rem(r, 2), rows // 2
    sibling = {"row": r + 1 - 2 * core}
    relay = cols == 4
    middle = lax.rem(lax.div(c + 1, 2), 2)
    inner, outer = middle == 1, middle == 0

    loads = [
        pltpu.make_async_copy(a, b, load.at[i])
        for i, (a, b) in enumerate(((w_hbm, w_ref), (t_hbm.at[pl.ds(0, t_all.shape[1])], t_all.at[0]), (p_hbm, p_ref), (l_hbm, l_ref)))
    ]
    loads += [
        pltpu.make_async_copy(t_hbm.at[pl.ds(h * t_all.shape[1], t_all.shape[1])], t_all.at[h], load.at[3 + h])
        for h in range(1, PARTS)
    ]
    for one in loads:
        one.start()

    def far(k):
        return {"row": lax.rem(r + 2 * k, rows)}

    def col_peer(s):
        return {"col": partner(c, s)}

    barrier = pltpu.get_barrier_semaphore()
    for peer in [sibling] + [far(k) for k in range(1, chips)] + [col_peer(s) for s in range(1, cols)]:
        pl.semaphore_signal(barrier, inc=1, device_id=peer, device_id_type=MESH)
    pl.semaphore_wait(barrier, chips + cols - 1)

    def push(src, dst, ssem, rsem, peer):
        pltpu.make_async_remote_copy(
            src_ref=src, dst_ref=dst, send_sem=ssem, recv_sem=rsem, device_id=peer, device_id_type=MESH
        ).start()

    def drain(ref, sem):
        pltpu.make_async_copy(ref, ref, sem).wait()

    def at(s, h):
        return s * PARTS + h

    def forward(full, s, h, sems, semr):
        if relay and s == 2:
            @pl.when(inner)
            def _():
                push(full.at[at(2, h)], full.at[at(3, h)], sems.at[at(0, h)], semr.at[at(3, h)], col_peer(1))

    def spread(src, full, h, sems, semr):
        def one(s):
            push(src, full.at[at(s, h)], sems.at[at(s, h)], semr.at[at(s, h)], col_peer(s))

        if relay:
            one(2)
            pl.when(inner)(lambda: one(3))
            one(1)
        else:
            for s in range(1, cols):
                one(s)

    step = t_all.shape[1]
    for h in range(PARTS):
        spread(t_hbm.at[pl.ds(h * step, step)], t_all, h, t_s, t_r)

    def cross(value, part, sib, half, away, b, s1, r1, s2, r2):
        part[b] = value.astype(BF16).reshape(part.shape[1:])
        push(part.at[b, 1 - core], sib.at[b], s1.at[b], r1.at[b], sibling)
        drain(sib.at[b], r1.at[b])
        half[b] = (part[b, core].astype(F32) + sib[b].astype(F32)).astype(BF16)
        for k in range(1, chips):
            push(half.at[b], away.at[b, k - 1], s2.at[b], r2.at[b], far(k))

    def finish(half, away, full, b, r2, s3, r3):
        drain(away.at[b], r2.at[b])
        total = half[b].astype(F32)
        for k in range(chips - 1):
            total = total + away[b, k].astype(F32)
        full[b, core] = total.astype(BF16)
        push(full.at[b, core], full.at[b, core], s3.at[b], r3.at[b], sibling)
        drain(half.at[b], r3.at[b])

    def give(value, part, came, s, h, sems, semr):
        b = at(s, h)
        part[b] = value.astype(BF16)
        peer = col_peer(s)
        if relay and s == 2:
            peer = {"col": middle * partner(c, 2) + (1 - middle) * partner(c, 1)}
        if relay and s == 3:
            @pl.when(inner)
            def _():
                drain(came.at[at(2, h)], semr.at[at(2, h)])
                part[b] = (value + came[at(2, h)].astype(F32)).astype(BF16)
        push(part.at[b], came.at[b], sems.at[b], semr.at[b], peer)

    def collect(total, came, h, semr):
        for s in range(1, cols):
            b = at(s, h)
            if relay and s == 2:
                @pl.when(outer)
                def _():
                    drain(came.at[b], semr.at[b])
                total = total + jnp.where(outer, came[b].astype(F32), 0.0)
            else:
                drain(came.at[b], semr.at[b])
                total = total + came[b].astype(F32)
        return total

    def whole(full, b):
        return full[b].reshape(full.shape[1] * full.shape[2], full.shape[3])

    def m_make(s, h):
        b = at(s, h)
        if s:
            drain(t_all.at[b], t_r.at[b])
            forward(t_all, s, h, t_s, t_r)
        cross(contract(t_all[b], w_ref[...], 1, 1), m_part, m_sib, m_half, m_far, b, m1_s, m1_r, m2_s, m2_r)

    def m_use(s, h):
        b = at(s, h)
        finish(m_half, m_far, m_all, b, m2_r, m3_s, m3_r)
        part = contract(p_ref[...], whole(m_all, b), 1, 1)
        if s:
            give(part, l_part, l_recv, s, h, l_s, l_r)
        else:
            acc[h] = part

    def d_make(h):
        logits = collect(acc[h], l_recv, h, l_r)
        labels = l_ref[:, h * step:(h + 1) * step].astype(F32)
        d_all[at(0, h)] = (jax.nn.sigmoid(logits * factor) - labels).astype(BF16)
        spread(d_all.at[at(0, h)], d_all, h, d_s, d_r)

    def q_make(s, h):
        b = at(s, h)
        if s:
            drain(d_all.at[b], d_r.at[b])
            forward(d_all, s, h, d_s, d_r)
        cross(contract(d_all[b], p_ref[...], 0, 0), q_part, q_sib, q_half, q_far, b, q1_s, q1_r, q2_s, q2_r)

    def q_use(s, h):
        b = at(s, h)
        finish(q_half, q_far, q_all, b, q2_r, q3_s, q3_r)
        part = contract(whole(q_all, b), w_ref[...], 1, 0)
        if s:
            give(part, g_part, g_recv, s, h, g_s, g_r)
        else:
            g_part[b] = part.astype(BF16)

    for one in loads:
        one.wait()
    makes = {"m": m_make, "q": q_make}
    uses = {"m": m_use, "q": q_use}
    order = M_ORDER if relay else tuple(range(cols))
    late = Q_ORDER if relay else tuple(range(cols))
    work = [("m", s, h) for h in range(PARTS) for s in order]
    work += [("q", s, h) for h in range(PARTS) for s in late]
    waiting, left = [], {h: cols for h in range(PARTS)}
    made = set()

    def use_first():
        kind, s, h = waiting.pop(0)
        uses[kind](s, h)
        if kind == "m":
            left[h] -= 1

    def settle(h):
        if h not in made and left[h] == 0:
            made.add(h)
            d_make(h)

    for i, (kind, s, h) in enumerate(work):
        if kind == "q" and s == late[D_AFTER if h == 0 else 0]:
            for g in range(h + 2 if h + 1 < PARTS else h + 1):
                while left[g]:
                    use_first()
                settle(g)
        elif kind == "q" and h not in made:
            while left[h]:
                use_first()
            settle(h)
        if kind == "m" and h and s == order[D_EARLY]:
            while left[h - 1]:
                use_first()
            settle(h - 1)
        makes[kind](s, h)
        waiting.append((kind, s, h))
        if len(waiting) > 1:
            use_first()
    while waiting:
        use_first()

    blocks = [at(s, h) for s in range(cols) for h in range(PARTS)]
    total = contract(d_all[0], whole(m_all, 0), 1, 0)
    for b in blocks[1:]:
        total = total + contract(d_all[b], whole(m_all, b), 1, 0)
    gp_ref[...] = (total * factor).astype(BF16)
    total = contract(whole(q_all, 0), t_all[0], 0, 0)
    for b in blocks[1:]:
        total = total + contract(whole(q_all, b), t_all[b], 0, 0)
    gw_ref[...] = total * factor
    for h in range(PARTS):
        total = collect(g_part[at(0, h)].astype(F32), g_recv, h, g_r)
        gt_ref[pl.ds(h * step, step)] = (total * factor).astype(BF16)

    for s in range(cols):
        for h in range(PARTS):
            b = at(s, h)
            for away, half, s1, s2, s3 in ((m_far, m_half, m1_s, m2_s, m3_s), (q_far, q_half, q1_s, q2_s, q3_s)):
                drain(half.at[b], s1.at[b])
                drain(away.at[b], s2.at[b])
                drain(half.at[b], s3.at[b])
            if s:
                drain(l_part.at[b], l_s.at[b])
                drain(g_part.at[b], g_s.at[b])
                if not (relay and s == 3):
                    drain(d_all.at[b], d_s.at[b])
                    drain(t_all.at[b], t_s.at[b])
    if relay:
        @pl.when(inner)
        def _():
            for h in range(PARTS):
                for full, sem in ((t_all, t_s), (d_all, d_s)):
                    drain(full.at[at(3, h)], sem.at[at(3, h)])
                    drain(full.at[at(2, h)], sem.at[at(0, h)])


def passed(a, b, c, x, y, z):
    x[...], y[...], z[...] = a[...], b[...], c[...]


def local(rows, cols, programs, tests, weight, labels):
    (pr, eb), (tb, fb) = programs.shape, tests.shape
    blocks, step, chips = cols * PARTS, tb // PARTS, rows // 2
    half = step // 2
    vmem, hbm = pl.BlockSpec(memory_space=pltpu.VMEM), pl.BlockSpec(memory_space=pl.ANY)
    block = lambda *shape: pltpu.VMEM((blocks, *shape), BF16)
    reduce = [block(2, half, eb), block(half, eb), block(half, eb), block(chips - 1, half, eb), block(2, half, eb)]
    outs = pl.pallas_call(
        functools.partial(kernel, rows, cols),
        out_shape=(
            jax.ShapeDtypeStruct((pr, eb), BF16),
            jax.ShapeDtypeStruct((tb, fb), BF16),
            jax.ShapeDtypeStruct((eb, fb), F32),
        ),
        in_specs=[hbm] * 4,
        out_specs=(vmem,) * 3,
        scratch_shapes=[
            pltpu.VMEM((pr, eb), BF16), pltpu.VMEM((eb, fb), BF16), pltpu.VMEM((pr, tb), jnp.int32),
            block(step, fb),
            *reduce,
            block(pr, step), block(pr, step),
            block(pr, step),
            *reduce,
            block(step, fb), block(step, fb),
            pltpu.VMEM((PARTS, pr, step), F32),
            pltpu.SemaphoreType.DMA((3 + PARTS,)),
            pltpu.SemaphoreType.DMA((10, blocks)),
            pltpu.SemaphoreType.DMA((10, blocks)),
        ],
        compiler_params=pltpu.CompilerParams(collective_id=0, has_side_effects=True),
    )(programs, tests, weight, labels)
    return pl.pallas_call(
        passed,
        out_shape=tuple(jax.ShapeDtypeStruct(x.shape, x.dtype) for x in outs),
        in_specs=[vmem] * 3,
        out_specs=(vmem,) * 3,
    )(*outs)


def solution(mesh):
    placed = (
        P(("grp", "row"), "col"),
        P(("grp", "col"), "row"),
        P("col", "row"),
        P(("grp", "row"), "col"),
    )
    return jax.shard_map(
        functools.partial(local, mesh.shape["row"], mesh.shape["col"]),
        mesh=mesh,
        in_specs=placed,
        out_specs=(P(("grp", "row"), "col"), P(("grp", "col"), "row"), P(("grp", "col"), "row")),
        check_vma=False,
    )
```
